256 devices in a mesh: row: 16 (over x, z_lo, core), col: 16 (over y, z_hi).
Axes of the slice: x: 4, y: 4, z: 8 (z_hi: 4, z_lo: 2; z = z_hi * 2 + z_lo), core: 2. Of those that a mesh axis runs over, the one named last changes fastest.
Arguments:
- ancestor_inverse: bfloat16 [32768, 32768], P('row', 'col'), may hold values from -0.03125 to 0.03125
- panel: bfloat16 [32768, 512], P(('row', 'col')), may hold values from -0.75 to 0.75
- structure: int32 [2, 128], replicated, may hold values 0 or 1
- diag_inverse: float32 [2, 256, 256], replicated, may hold values from -6 to 6
Outputs:
- upper: bfloat16 [32768, 512], P(('row', 'col'))
- diagonal: float32 [2, 256, 256], replicated
The draws below stay inside these ranges and needn't reach their ends.
All inputs are finite; a program needn't handle non-finite values.
Results may differ from the reference program's by a relative error of at most 0.0014.
Values may be sent and summed in bfloat16 or wider, within the bound.
A program may use at most 64 MiB of HBM per device.

```python
import jax
import jax.numpy as jnp
from jax import lax

WIDTH = 256
SNODES = 2
BLOCKS = 128
ROWS = 32768


def touch_ends(entries, key, low, high):
    longest = entries.shape.index(max(entries.shape))
    spots = []
    for shift in (0, 1):
        where = [jax.random.randint(jax.random.fold_in(key, axis), (), 0, length) for axis, length in enumerate(entries.shape)]
        where[longest] = (where[longest] + shift) % entries.shape[longest]
        spots.append(tuple(where))
    return entries.at[spots[0]].set(low).at[spots[1]].set(high)


def level_of(rng, dims, cuts, least, high):
    loudness, own = 1.0, jax.random.fold_in(rng, 6)
    for dim, parts in cuts:
        steps = jnp.exp(jax.random.uniform(jax.random.fold_in(own, dim), (parts,), jnp.float32, least / len(cuts), high / len(cuts)))
        loudness = loudness * jnp.repeat(steps, dims[dim] // parts).reshape([-1 if axis == dim else 1 for axis in range(len(dims))])
    return loudness


def noise(own_key, extent, spread, bound, split=(), held_as=jnp.bfloat16):
    factor_of = level_of(own_key, extent, split, -0.22, 0.18) if split else 1.0
    array = jax.random.normal(own_key, extent, jnp.float32) * spread * factor_of
    return jnp.minimum(jnp.maximum(array, -bound), bound).astype(held_as)


def setup_inputs(seed: int = 0) -> dict:
    key_list = jax.random.split(jax.random.key(seed), 5)
    return {
        "ancestor_inverse": noise(key_list[0], (ROWS, ROWS), ROWS ** -0.5, 0.03125, ((0, 16), (1, 16))),
        "panel": noise(key_list[1], (ROWS, SNODES * WIDTH), 0.125, 0.75, ((0, 256),)),
        "structure": touch_ends((jax.random.randint(key_list[2], (SNODES, BLOCKS), 0, 4) < 3).astype(jnp.int32), jax.random.fold_in(key_list[2], 1), 0, 1),
        "diag_inverse": noise(key_list[3], (SNODES, WIDTH, WIDTH), 1.0, 6.0, (), jnp.float32),
    }


def reference(ancestor_inverse, panel, structure, diag_inverse):
    keeps = jnp.repeat(structure.T.astype(jnp.float32), WIDTH, axis=0)
    keep = jnp.repeat(keeps, WIDTH, axis=1)
    masked = panel * keep.astype(jnp.bfloat16)
    full = -jnp.dot(ancestor_inverse, masked, preferred_element_type=jnp.float32)
    full = full * keep
    upper = full.astype(jnp.bfloat16)
    lower_f = masked.astype(jnp.float32).reshape(ROWS, SNODES, WIDTH)
    upper_f = full.reshape(ROWS, SNODES, WIDTH)
    update = jnp.einsum("mkw,mkv->kwv", lower_f, upper_f, precision=lax.Precision.HIGHEST)
    return upper, diag_inverse - update
```

```python
import jax
import jax.numpy as jnp
from jax import lax
from jax.sharding import PartitionSpec as P


def row_keep(begin_row, length, structure, blk_width):
    blocks_all = structure.shape[1]
    indices = begin_row + jnp.arange(length, dtype=jnp.int32)
    owners = indices // blk_width
    onehot = (owners[:, None] == jnp.arange(blocks_all, dtype=jnp.int32)[None, :]).astype(
        jnp.float32
    )
    keeps = jnp.dot(onehot, structure.T.astype(jnp.float32), preferred_element_type=jnp.float32)
    return jnp.repeat(keeps, blk_width, axis=1)


def diag_part(lower, upper_rows, blk_width):
    snodes = upper_rows.shape[1] // blk_width
    lower_f = lower.astype(jnp.float32).reshape(lower.shape[0], snodes, blk_width)
    upper_f = upper_rows.reshape(upper_rows.shape[0], snodes, blk_width)
    return jnp.einsum("mkw,mkv->kwv", lower_f, upper_f, precision=lax.Precision.HIGHEST)


def local(ancestor_inverse, panel, structure, diag_inverse):
    blk_width = diag_inverse.shape[1]
    row_count = lax.axis_size("row")
    col_count = lax.axis_size("col")
    row_index = lax.axis_index("row")
    col_index = lax.axis_index("col")
    piece_rows = panel.shape[0]
    begin_own = (row_index * col_count + col_index) * piece_rows
    keep_own = row_keep(begin_own, piece_rows, structure, blk_width)
    masked = panel * keep_own.astype(jnp.bfloat16)
    flip = [(r * col_count + c, c * row_count + r) for r in range(row_count) for c in range(col_count)]
    moved = lax.ppermute(masked, ("row", "col"), flip)
    col_block = lax.all_gather(moved, "row", axis=0, tiled=True)
    partial_rows = -jnp.dot(ancestor_inverse, col_block, preferred_element_type=jnp.float32)
    own_rows = lax.psum_scatter(partial_rows, "col", scatter_dimension=0, tiled=True)
    diag_sum = lax.psum(diag_part(masked, own_rows, blk_width), ("row", "col"))
    upper = (own_rows * keep_own).astype(jnp.bfloat16)
    diagonal = diag_inverse - diag_sum
    return (upper, diagonal)


def solution(mesh):
    return jax.shard_map(
        local,
        mesh=mesh,
        in_specs=(P("row", "col"), P(("row", "col"), None), P(), P()),
        out_specs=(P(("row", "col"), None), P()),
        check_vma=False,
    )
```

```python
import functools

import jax
import jax.numpy as jnp
from jax import lax
from jax.experimental import pallas as pl
from jax.experimental.pallas import tpu as pltpu
from jax.sharding import PartitionSpec as P

MESH = pl.DeviceIdType.MESH
F32 = jnp.float32
BF16 = jnp.bfloat16
I16 = jnp.int16
WIDE = 256
PIECE = 128
ROUND = 12582912.0


def encode(tile, ref):
    rows = tile.shape[0]
    top = jnp.maximum(jnp.max(jnp.abs(tile), axis=0, keepdims=True), 1e-30)
    power = jnp.floor(jnp.log2(top)) - 13.0
    scaled = tile * jnp.exp2(-power)
    whole = (scaled + ROUND) - ROUND
    ref[0:rows, :] = whole.astype(jnp.int32).astype(I16)
    ref[rows:rows + 16, :] = jnp.broadcast_to(power, (16, tile.shape[1])).astype(jnp.int32).astype(I16)


def decode(ref, first=0, count=None):
    rows = ref.shape[0] - 16
    count = rows if count is None else count
    power = ref[rows:rows + 16, :].astype(jnp.int32).astype(F32)
    scale = jnp.exp2(power)[0:1, :]
    return ref[first:first + count, :].astype(jnp.int32).astype(F32) * scale


def kernel(a_hbm, panel_ref, structure_ref, dinv_hbm, upper_ref, diag_ref,
           a_v, own, neg, xb, sy, ry, sz, rz, ss, dsend, drecv, xs, xr, ys, yr, zr,
           dg, dchunk, lsem, ssem, rsem):
    R = lax.axis_index("row")
    C = lax.axis_index("col")
    x, zl, k = R // 4, (R // 2) % 2, R % 2
    y, zh = C // 4, C % 4
    z = zh * 2 + zl

    def at(dx=0, dy=0, dz=0, dzh=0, flip=False, sib=False):
        x2 = (x + dx) % 4
        y2 = (y + dy) % 4
        z2 = (z + dz + 2 * dzh) % 8
        zl2 = 1 - z2 % 2 if flip else z2 % 2
        k2 = 1 - k if sib else k
        return (x2 * 4 + zl2 * 2 + k2, y2 * 4 + z2 // 2)

    off_diagonal = R != C
    ids = {}
    sends = []

    def copy(name, src, dst, dev):
        i = ids.setdefault(name, len(ids))
        return pltpu.make_async_remote_copy(
            src_ref=src, dst_ref=dst, send_sem=ssem.at[i], recv_sem=rsem.at[i],
            device_id=dev, device_id_type=MESH)

    def send(name, src, dst, dev):
        cp = copy(name, src, dst, dev)
        cp.start()
        sends.append(cp)

    def recv(name, dst):
        copy(name, dst, dst, at(sib=True)).wait_recv()

    loads = []
    for t in range(8):
        cp = pltpu.make_async_copy(a_hbm.at[pl.ds(t * 256, 256), :], a_v.at[pl.ds(t * 256, 256), :], lsem.at[t])
        cp.start()
        loads.append(cp)
    mine16 = pl.multiple_of(x * 64 + y * 16, 16)
    cp = pltpu.make_async_copy(dinv_hbm.at[k, pl.ds(mine16, 16), :], dchunk, lsem.at[8])
    cp.start()
    loads.append(cp)

    block = (R * 16 + C) // 2
    keeps = []
    for q in range(2):
        keep = structure_ref[q, block].astype(F32)
        keeps.append(keep)
        m = panel_ref[:, q * WIDE:(q + 1) * WIDE].astype(F32) * keep
        own[q] = m.astype(BF16)
        neg[q] = (-m).astype(BF16)

    barrier = pltpu.get_barrier_semaphore()
    partners = [at(sib=True)]
    partners += [at(dx=d) for d in (1, 2, 3)]
    partners += [at(dy=d) for d in (1, 2, 3)]
    partners += [at(dz=d) for d in range(1, 8)]
    for dev in partners:
        pl.semaphore_signal(barrier, inc=1, device_id=dev, device_id_type=MESH)

    @pl.when(off_diagonal)
    def _():
        pl.semaphore_signal(barrier, inc=1, device_id=(C, R), device_id_type=MESH)
        pl.semaphore_wait(barrier, len(partners) + 1)

    @pl.when(jnp.logical_not(off_diagonal))
    def _():
        pl.semaphore_wait(barrier, len(partners))

    def slot(q, s):
        return xb.at[q, pl.ds(pl.multiple_of(s * PIECE, PIECE), PIECE), :]

    def half(q, s, h):
        return xb.at[q, pl.ds(pl.multiple_of(s * PIECE + h * 64, 64), 64), :]

    def lane(dx, n):
        return ((x + dx) % 4) * 4 + (zl + n) % 2 * 2 + k

    for q in range(2):
        first = copy(("g1", q), neg.at[q], slot(q, C), (C, R))

        @pl.when(off_diagonal)
        def _():
            first.start()

        @pl.when(jnp.logical_not(off_diagonal))
        def _():
            xb[q, pl.ds(pl.multiple_of(R * PIECE, PIECE), PIECE), :] = neg[q]

    def spread(q, n, s, dxs, i):
        if 1 in dxs:
            send(("gxp", q, n), slot(q, s), slot(q, s), at(dx=1))
        if -1 in dxs:
            send(("gxm", q, n), slot(q, s), slot(q, s), at(dx=-1))
        send(("gs", q, i), slot(q, s), slot(q, s), at(sib=True))

    def s1(q):
        @pl.when(off_diagonal)
        def _():
            recv(("g1", q), slot(q, R))
        send(("gz", q), slot(q, R), slot(q, R), at(flip=True))
        spread(q, 0, lane(0, 0), (1, -1), 0)

    def s2(q):
        recv(("gz", q), slot(q, lane(0, 1)))
        spread(q, 1, lane(0, 1), (1, -1), 1)

    def s3(q, n):
        s = lane(1, n)
        recv(("gxm", q, n), slot(q, s))
        send(("ghm", q, n), half(q, s, 0), half(q, s, 0), at(dx=-1))
        spread(q, n, s, (), 2 + n)
        s = lane(-1, n)
        recv(("gxp", q, n), slot(q, s))
        send(("ghp", q, n), half(q, s, 1), half(q, s, 1), at(dx=1))
        spread(q, n, s, (), 4 + n)

    def s5(q, n):
        s = lane(2, n)
        recv(("ghm", q, n), half(q, s, 0))
        recv(("ghp", q, n), half(q, s, 1))
        spread(q, n, s, (), 6 + n)

    def s6(q):
        for n in range(2):
            for i, dx in ((0, 0), (2, 1), (4, -1), (6, 2)):
                s = ((x + dx) % 4) * 4 + (zl + n) % 2 * 2 + 1 - k
                recv(("gs", q, i + n), slot(q, s))

    def tile(q, dy, u):
        r0 = pl.multiple_of(((y + dy) % 4) * 512 + u * 256, 256)
        return jnp.dot(a_v[pl.ds(r0, 256), :], xb[q], preferred_element_type=F32)

    def y_send(q, i, value, dy):
        encode(value, sy.at[q, i])
        send(("y", q, i), sy.at[q, i], ry.at[q, i], at(dy=dy))

    def y_first(q, after):
        y_send(q, 0, tile(q, 2, 0), 1)
        after(0)
        y_send(q, 1, tile(q, 2, 1), -1)
        after(1)
        y_send(q, 2, tile(q, 1, 1), 1)
        y_send(q, 3, tile(q, -1, 0), -1)

    def y_own(q):
        for u in range(2):
            ss[q, u * 256:(u + 1) * 256, :] = tile(q, 0, u)

    def y_relay(q):
        t = tile(q, 1, 0)
        recv(("y", q, 0), ry.at[q, 0])
        y_send(q, 4, t + decode(ry.at[q, 0]), 1)
        t = tile(q, -1, 1)
        recv(("y", q, 1), ry.at[q, 1])
        y_send(q, 5, t + decode(ry.at[q, 1]), -1)

    def y_last(q):
        for i in (2, 3, 4, 5):
            recv(("y", q, i), ry.at[q, i])
        ss[q, 0:256, :] = ss[q, 0:256, :] + decode(ry.at[q, 3]) + decode(ry.at[q, 4])
        ss[q, 256:512, :] = ss[q, 256:512, :] + decode(ry.at[q, 2]) + decode(ry.at[q, 5])

    def z_ref(buf, q, i):
        return buf.at[q, i, pl.ds(0, 80 if i < 2 else 144), :]

    def z_send(q, i, value, dzh):
        encode(value, z_ref(sz, q, i))
        send(("z", q, i), z_ref(sz, q, i), z_ref(rz, q, i), at(dzh=dzh))

    def z_rows(q, d, start, count):
        r0 = pl.multiple_of(((zh + d) % 4) * PIECE + start, 64)
        return ss[q, pl.ds(r0, count), :]

    def z_first(q):
        z_send(q, 0, z_rows(q, 2, 0, 64), 1)
        z_send(q, 1, z_rows(q, 2, 64, 64), -1)

    def z_relay(q):
        recv(("z", q, 0), z_ref(rz, q, 0))
        v = jnp.concatenate([z_rows(q, 1, 0, 64) + decode(z_ref(rz, q, 0)), z_rows(q, 1, 64, 64)], axis=0)
        z_send(q, 2, v, 1)
        recv(("z", q, 1), z_ref(rz, q, 1))
        v = jnp.concatenate([z_rows(q, -1, 0, 64), z_rows(q, -1, 64, 64) + decode(z_ref(rz, q, 1))], axis=0)
        z_send(q, 3, v, -1)

    def z_last(q):
        recv(("z", q, 2), z_ref(rz, q, 2))
        recv(("z", q, 3), z_ref(rz, q, 3))
        full = z_rows(q, 0, 0, PIECE) + decode(z_ref(rz, q, 2)) + decode(z_ref(rz, q, 3))
        upper_ref[:, q * WIDE:(q + 1) * WIDE] = (full * keeps[q]).astype(BF16)
        high = full.astype(BF16)
        low = (full - high.astype(F32)).astype(BF16)
        dims = (((0,), (0,)), ((), ()))
        dsend[q] = (lax.dot_general(own[q], high, dims, preferred_element_type=F32)
                    + lax.dot_general(own[q], low, dims, preferred_element_type=F32))

    s1(0)
    s1(1)
    s2(0)
    s3(0, 0)
    s2(1)
    s3(1, 0)
    s3(0, 1)
    s5(0, 0)
    s3(1, 1)
    s5(0, 1)
    s5(1, 0)
    for cp in loads:
        cp.wait()
    s6(0)

    def between(i):
        if i == 0:
            s5(1, 1)

    y_first(0, between)
    y_own(0)
    y_relay(0)
    s6(1)
    y_first(1, lambda i: None)
    y_own(1)
    y_last(0)
    z_first(0)
    y_relay(1)
    z_relay(0)
    z_last(0)
    y_last(1)
    z_first(1)
    z_relay(1)
    z_last(1)

    mate = at(sib=True)
    send("core", dsend.at[1 - k], drecv, mate)
    recv("core", drecv)
    xs[...] = dsend[k] + drecv[...]
    for d in (1, 2, 3):
        send(("dx", d), xs.at[pl.ds(pl.multiple_of(((x + d) % 4) * 64, 64), 64), :], xr.at[d - 1], at(dx=d))
    total = xs[pl.ds(pl.multiple_of(x * 64, 64), 64), :]
    for d in (1, 2, 3):
        recv(("dx", d), xr.at[d - 1])
        total = total + xr[d - 1]
    ys[...] = total
    for d in (1, 2, 3):
        send(("dy", d), ys.at[pl.ds(pl.multiple_of(((y + d) % 4) * 16, 16), 16), :], yr.at[d - 1], at(dy=d))
    total = ys[pl.ds(pl.multiple_of(y * 16, 16), 16), :]
    for d in (1, 2, 3):
        recv(("dy", d), yr.at[d - 1])
        total = total + yr[d - 1]
    zr[z] = total
    for d in range(1, 8):
        send(("dz", d), zr.at[z], zr.at[z], at(dz=d))
    for d in range(1, 8):
        recv(("dz", d), zr.at[(z + 8 - d) % 8])
    total = zr[0]
    for i in range(1, 8):
        total = total + zr[i]
    part = dg.at[k, pl.ds(mine16, 16), :]
    dg[k, pl.ds(mine16, 16), :] = dchunk[...] - total
    for d in (1, 2, 3):
        send(("ay", d), part, part, at(dy=d))
    for d in (1, 2, 3):
        recv(("ay", d), dg.at[k, pl.ds(pl.multiple_of(x * 64 + ((y + 4 - d) % 4) * 16, 16), 16), :])
    part = dg.at[k, pl.ds(pl.multiple_of(x * 64, 64), 64), :]
    for d in (1, 2, 3):
        send(("ax", d), part, part, at(dx=d))
    for d in (1, 2, 3):
        recv(("ax", d), dg.at[k, pl.ds(pl.multiple_of(((x + 4 - d) % 4) * 64, 64), 64), :])
    send("ac", dg.at[k], dg.at[k], mate)
    recv("ac", dg.at[1 - k])
    diag_ref[...] = dg[...]

    for q in range(2):
        cp = copy(("g1", q), neg.at[q], slot(q, C), (C, R))

        @pl.when(off_diagonal)
        def _():
            cp.wait_send()
    for cp in sends:
        cp.wait_send()
    assert len(ids) <= COPIES, len(ids)


COPIES = 96


def local(ancestor_inverse, panel, structure, diag_inverse):
    vmem = pl.BlockSpec(memory_space=pltpu.VMEM)
    hbm = pl.BlockSpec(memory_space=pl.ANY)
    return pl.pallas_call(
        kernel,
        out_shape=(jax.ShapeDtypeStruct(panel.shape, BF16), jax.ShapeDtypeStruct(diag_inverse.shape, F32)),
        in_specs=[hbm, vmem, pl.BlockSpec(memory_space=pltpu.SMEM), hbm],
        out_specs=(vmem, vmem),
        scratch_shapes=[
            pltpu.VMEM((2048, 2048), BF16),
            pltpu.VMEM((2, PIECE, WIDE), BF16),
            pltpu.VMEM((2, PIECE, WIDE), BF16),
            pltpu.VMEM((2, 2048, WIDE), BF16),
            pltpu.VMEM((2, 6, 272, WIDE), I16),
            pltpu.VMEM((2, 6, 272, WIDE), I16),
            pltpu.VMEM((2, 4, 144, WIDE), I16),
            pltpu.VMEM((2, 4, 144, WIDE), I16),
            pltpu.VMEM((2, 512, WIDE), F32),
            pltpu.VMEM((2, WIDE, WIDE), F32),
            pltpu.VMEM((WIDE, WIDE), F32),
            pltpu.VMEM((WIDE, WIDE), F32),
            pltpu.VMEM((3, 64, WIDE), F32),
            pltpu.VMEM((64, WIDE), F32),
            pltpu.VMEM((3, 16, WIDE), F32),
            pltpu.VMEM((8, 16, WIDE), F32),
            pltpu.VMEM((2, WIDE, WIDE), F32),
            pltpu.VMEM((16, WIDE), F32),
            pltpu.SemaphoreType.DMA((9,)),
            pltpu.SemaphoreType.DMA((COPIES,)),
            pltpu.SemaphoreType.DMA((COPIES,)),
        ],
        compiler_params=pltpu.CompilerParams(
            collective_id=0, has_side_effects=True, vmem_limit_bytes=60 * 1024 * 1024),
    )(ancestor_inverse, panel, structure, diag_inverse)


def solution(mesh):
    return jax.shard_map(
        local,
        mesh=mesh,
        in_specs=(P("row", "col"), P(("row", "col"), None), P(), P()),
        out_specs=(P(("row", "col"), None), P()),
        check_vma=False,
    )
```

```python
import functools

import jax
import jax.numpy as jnp
from jax import lax
from jax.experimental import pallas as pl
from jax.experimental.pallas import tpu as pltpu
from jax.sharding import PartitionSpec as P

MESH = pl.DeviceIdType.MESH
F32 = jnp.float32
BF16 = jnp.bfloat16
I16 = jnp.int16
WIDE = 256
PIECE = 128
ROUND = 12582912.0


def encode(tile, ref):
    rows = tile.shape[0]
    top = jnp.maximum(jnp.max(jnp.abs(tile), axis=0, keepdims=True), 1e-30)
    power = jnp.floor(jnp.log2(top)) - 13.0
    scaled = tile * jnp.exp2(-power)
    whole = (scaled + ROUND) - ROUND
    ref[0:rows, :] = whole.astype(jnp.int32).astype(I16)
    ref[rows:rows + 16, :] = jnp.broadcast_to(power, (16, tile.shape[1])).astype(jnp.int32).astype(I16)


def decode(ref, first=0, count=None):
    rows = ref.shape[0] - 16
    count = rows if count is None else count
    power = ref[rows:rows + 16, :].astype(jnp.int32).astype(F32)
    scale = jnp.exp2(power)[0:1, :]
    return ref[first:first + count, :].astype(jnp.int32).astype(F32) * scale


def kernel(a_hbm, panel_ref, structure_ref, dinv_hbm, upper_ref, diag_ref,
           a_v, own, neg, xb, mg, sy, ry, sz, rz, ss, dsend, drecv, xs, xr, zr,
           dg, dchunk, lsem, ssem, rsem):
    R = lax.axis_index("row")
    C = lax.axis_index("col")
    x, zl, k = R // 4, (R // 2) % 2, R % 2
    y, zh = C // 4, C % 4
    z = zh * 2 + zl

    def at(dx=0, dy=0, dz=0, dzh=0, flip=False, sib=False):
        x2 = (x + dx) % 4
        y2 = (y + dy) % 4
        z2 = (z + dz + 2 * dzh) % 8
        zl2 = 1 - z2 % 2 if flip else z2 % 2
        k2 = 1 - k if sib else k
        return (x2 * 4 + zl2 * 2 + k2, y2 * 4 + z2 // 2)

    def holder(r, j):
        xs_, zls, ks = r // 4, (r // 2) % 2, r % 2
        i = (j % 4 - 2 * zls - ks + 8) % 4
        x2 = (2 * xs_ + 6 - j // 4) % 4
        upper_half = i // 2
        zl2 = jnp.where(zls == 0, (i + 1) // 2 % 2, 1 - upper_half)
        k2 = jnp.where(zls == 0, upper_half, i % 2)
        return x2 * 4 + zl2 * 2 + k2

    def piece(r, h):
        xs_, zls, ks = r // 4, (r // 2) % 2, r % 2
        x2, zl2, k2 = h // 4, (h // 2) % 2, h % 2
        i = jnp.where(zls == 0, jnp.where(zl2 == 0, 3 * k2, 1 + k2), 2 * (1 - zl2) + k2)
        return (2 * xs_ + 6 - x2) % 4 * 4 + (i + 2 * zls + ks) % 4

    ids = {}
    sends = []

    def copy(name, src, dst, dev):
        i = ids.setdefault(name, len(ids))
        return pltpu.make_async_remote_copy(
            src_ref=src, dst_ref=dst, send_sem=ssem.at[i], recv_sem=rsem.at[i],
            device_id=dev, device_id_type=MESH)

    def send(name, src, dst, dev):
        cp = copy(name, src, dst, dev)
        cp.start()
        sends.append(cp)

    def recv(name, dst):
        copy(name, dst, dst, at(sib=True)).wait_recv()

    loads = []
    for t in range(8):
        cp = pltpu.make_async_copy(a_hbm.at[pl.ds(t * 256, 256), :], a_v.at[pl.ds(t * 256, 256), :], lsem.at[t])
        cp.start()
        loads.append(cp)
    mine8 = pl.multiple_of(k * 128 + x * 32 + y * 8, 8)
    cp = pltpu.make_async_copy(dinv_hbm.at[:, pl.ds(mine8, 8), :], dchunk, lsem.at[8])
    cp.start()
    loads.append(cp)

    block = (R * 16 + C) // 2
    keeps = []
    for q in range(2):
        keep = structure_ref[q, block].astype(F32)
        keeps.append(keep)
        m = panel_ref[:, q * WIDE:(q + 1) * WIDE].astype(F32) * keep
        own[q] = m.astype(BF16)
        neg[q] = (-m).astype(BF16)

    barrier = pltpu.get_barrier_semaphore()
    target = (holder(R, C), R)
    source = (C, piece(C, R))
    partners = [at(sib=True), source]
    plane = [(d // 4, d % 4) for d in range(1, 16)]
    partners += [at(dx=dx, dy=dy) for dx, dy in plane]
    partners += [at(dx=d, flip=True) for d in (1, 3)]
    partners += [at(dz=d) for d in range(1, 8)]
    for dev in partners:
        pl.semaphore_signal(barrier, inc=1, device_id=dev, device_id_type=MESH)
    pl.semaphore_wait(barrier, len(partners))

    def slot(q, s):
        return xb.at[q, pl.ds(pl.multiple_of(s * PIECE, PIECE), PIECE), :]

    def half(q, s, h):
        return xb.at[q, pl.ds(pl.multiple_of(s * PIECE + h * 64, 64), 64), :]

    def lane(dx, n, other=False):
        return piece(C, ((x + dx) % 4) * 4 + (zl + n) % 2 * 2 + (1 - k if other else k))

    for q in range(2):
        send(("g1", q), neg.at[q], slot(q, C), target)

    def share(q, s, i):
        send(("gs", q, i), slot(q, s), slot(q, s), at(sib=True))

    def s1(q):
        s = lane(0, 0)
        recv(("g1", q), slot(q, s))
        names = [("xp", at(dx=1)), ("xm", at(dx=-1)), ("z", at(flip=True))]
        if q == 0:
            names += [("zp", at(dx=1, flip=True)), ("zm", at(dx=-1, flip=True))]
        for name, dev in names:
            send((name, q), slot(q, s), slot(q, s), dev)
        share(q, s, 0)

    def s2(q):
        s = lane(0, 1)
        recv(("z", q), slot(q, s))
        if q == 1:
            send(("zp", q), slot(q, s), slot(q, s), at(dx=1))
            send(("zm", q), slot(q, s), slot(q, s), at(dx=-1))
        share(q, s, 1)

    def s3(q, n):
        s = lane(1, n)
        recv(("zm" if n else "xm", q), slot(q, s))
        send(("hm", q, n), half(q, s, 0), half(q, s, 0), at(dx=-1))
        share(q, s, 2 + n)
        s = lane(-1, n)
        recv(("zp" if n else "xp", q), slot(q, s))
        send(("hp", q, n), half(q, s, 1), half(q, s, 1), at(dx=1))
        share(q, s, 4 + n)

    def s5(q, n):
        s = lane(2, n)
        recv(("hm", q, n), half(q, s, 0))
        recv(("hp", q, n), half(q, s, 1))
        share(q, s, 6 + n)

    def s6(q):
        for n in range(2):
            for i, dx in ((0, 0), (2, 1), (4, -1), (6, 2)):
                recv(("gs", q, i + n), slot(q, lane(dx, n, True)))

    def m_rows(d):
        return mg.at[:, pl.ds(pl.multiple_of(((zh + d) % 4) * PIECE, PIECE), PIECE), :]

    def m_send():
        for q in range(2):
            mg[q, pl.ds(pl.multiple_of(zh * PIECE, PIECE), PIECE), :] = own[q]
        for d in (1, 2, 3):
            send(("m", d), own, m_rows(0), at(dzh=d))

    def m_recv():
        for d in (1, 2, 3):
            recv(("m", d), m_rows(4 - d))

    def tile(q, dy, u):
        r0 = pl.multiple_of(((y + dy) % 4) * 512 + u * 256, 256)
        return jnp.dot(a_v[pl.ds(r0, 256), :], xb[q], preferred_element_type=F32)

    def y_send(q, i, value, dy):
        encode(value, sy.at[q, i])
        send(("y", q, i), sy.at[q, i], ry.at[q, i], at(dy=dy))

    def y_first(q, after):
        y_send(q, 0, tile(q, 2, 0), 1)
        after(0)
        y_send(q, 1, tile(q, 2, 1), -1)
        after(1)
        y_send(q, 2, tile(q, 1, 1), 1)
        y_send(q, 3, tile(q, -1, 0), -1)

    def y_own(q):
        for u in range(2):
            ss[q, u * 256:(u + 1) * 256, :] = tile(q, 0, u)

    def y_relay(q):
        t = tile(q, 1, 0)
        recv(("y", q, 0), ry.at[q, 0])
        y_send(q, 4, t + decode(ry.at[q, 0]), 1)
        t = tile(q, -1, 1)
        recv(("y", q, 1), ry.at[q, 1])
        y_send(q, 5, t + decode(ry.at[q, 1]), -1)

    def y_last(q):
        for i in (2, 3, 4, 5):
            recv(("y", q, i), ry.at[q, i])
        ss[q, 0:256, :] = ss[q, 0:256, :] + decode(ry.at[q, 3]) + decode(ry.at[q, 4])
        ss[q, 256:512, :] = ss[q, 256:512, :] + decode(ry.at[q, 2]) + decode(ry.at[q, 5])

    def z_ref(buf, q, i):
        return buf.at[q, i, pl.ds(0, 80 if i < 2 else 144), :]

    def z_send(q, i, value, dzh):
        encode(value, z_ref(sz, q, i))
        send(("z", q, i), z_ref(sz, q, i), z_ref(rz, q, i), at(dzh=dzh))

    def z_rows(q, d, start, count):
        r0 = pl.multiple_of(((zh + d) % 4) * PIECE + start, 64)
        return ss[q, pl.ds(r0, count), :]

    def z_first(q):
        z_send(q, 0, z_rows(q, 2, 0, 64), 1)
        z_send(q, 1, z_rows(q, 2, 64, 64), -1)

    def z_relay(q):
        recv(("z", q, 0), z_ref(rz, q, 0))
        v = jnp.concatenate([z_rows(q, 1, 0, 64) + decode(z_ref(rz, q, 0)), z_rows(q, 1, 64, 64)], axis=0)
        z_send(q, 2, v, 1)
        recv(("z", q, 1), z_ref(rz, q, 1))
        v = jnp.concatenate([z_rows(q, -1, 0, 64), z_rows(q, -1, 64, 64) + decode(z_ref(rz, q, 1))], axis=0)
        z_send(q, 3, v, -1)

    def z_last(q):
        recv(("z", q, 2), z_ref(rz, q, 2))
        recv(("z", q, 3), z_ref(rz, q, 3))
        full = z_rows(q, 0, 0, PIECE) + decode(z_ref(rz, q, 2)) + decode(z_ref(rz, q, 3))
        upper_ref[:, q * WIDE:(q + 1) * WIDE] = (full * keeps[q]).astype(BF16)

    mate = at(sib=True)

    def rows(start, count):
        return pl.ds(pl.multiple_of(start, 8), count)

    def d_core(q):
        dims = (((0,), (0,)), ((), ()))
        part = ss[q]
        high = part.astype(BF16)
        low = (part - high.astype(F32)).astype(BF16)
        dsend[q] = (lax.dot_general(mg[q], high, dims, preferred_element_type=F32)
                    + lax.dot_general(mg[q], low, dims, preferred_element_type=F32))
        send(("core", q), dsend.at[q, rows((1 - k) * 128, 128), :], drecv.at[q], mate)

    def d_plane(q):
        recv(("core", q), drecv.at[q])
        xs[q] = dsend[q, rows(k * 128, 128), :] + drecv[q]
        for i, (dx, dy) in enumerate(plane):
            r0 = ((x + dx) % 4) * 32 + ((y + dy) % 4) * 8
            send(("dp", q, i), xs.at[q, rows(r0, 8), :], xr.at[q, i], at(dx=dx, dy=dy))

    def d_z(q):
        total = xs[q, rows(x * 32 + y * 8, 8), :]
        for i in range(15):
            recv(("dp", q, i), xr.at[q, i])
            total = total + xr[q, i]
        zr[q, z] = total
        for d in range(1, 8):
            send(("dz", q, d), zr.at[q, z], zr.at[q, z], at(dz=d))

    def d_back(q):
        for d in range(1, 8):
            recv(("dz", q, d), zr.at[q, (z + 8 - d) % 8])
        total = zr[q, 0]
        for i in range(1, 8):
            total = total + zr[q, i]
        dg[q, pl.ds(mine8, 8), :] = dchunk[q] - total
        part = dg.at[q, pl.ds(mine8, 8), :]
        for i, (dx, dy) in enumerate(plane):
            send(("ap", q, i), part, part, at(dx=dx, dy=dy))

    def d_back_core(q):
        for i, (dx, dy) in enumerate(plane):
            r0 = k * 128 + ((x + 4 - dx) % 4) * 32 + ((y + 4 - dy) % 4) * 8
            recv(("ap", q, i), dg.at[q, rows(r0, 8), :])
        part = dg.at[q, rows(k * 128, 128), :]
        send(("ac", q), part, part, mate)

    def d_end(q):
        recv(("ac", q), dg.at[q, rows((1 - k) * 128, 128), :])
        diag_ref[q] = dg[q]

    s1(0)
    s1(1)
    s3(0, 0)
    s2(1)
    s3(0, 1)
    s2(0)
    s3(1, 0)
    for cp in loads:
        cp.wait()
    s5(0, 0)
    s3(1, 1)
    s5(0, 1)
    s6(0)
    y_first(0, lambda i: m_send() if i == 0 else s5(1, 0))
    y_own(0)
    s5(1, 1)
    y_relay(0)
    s6(1)
    y_first(1, lambda i: None)
    y_own(1)
    m_recv()
    y_last(0)
    d_core(0)
    z_first(0)
    y_relay(1)
    d_plane(0)
    z_relay(0)
    z_last(0)
    d_z(0)
    y_last(1)
    d_core(1)
    z_first(1)
    d_plane(1)
    d_back(0)
    z_relay(1)
    d_z(1)
    z_last(1)
    d_back_core(0)
    d_back(1)
    d_end(0)
    d_back_core(1)
    d_end(1)
    for cp in sends:
        cp.wait_send()
    assert len(ids) <= COPIES, len(ids)


def place(upper_ref, diag_ref, upper_out, diag_out):
    upper_out[...] = upper_ref[...]
    diag_out[...] = diag_ref[...]


COPIES = 160


def local(ancestor_inverse, panel, structure, diag_inverse):
    vmem = pl.BlockSpec(memory_space=pltpu.VMEM)
    hbm = pl.BlockSpec(memory_space=pltpu.HBM)
    upper, diagonal = pl.pallas_call(
        kernel,
        out_shape=(jax.ShapeDtypeStruct(panel.shape, BF16), jax.ShapeDtypeStruct(diag_inverse.shape, F32)),
        in_specs=[hbm, vmem, pl.BlockSpec(memory_space=pltpu.SMEM), hbm],
        out_specs=(vmem, vmem),
        scratch_shapes=[
            pltpu.VMEM((2048, 2048), BF16),
            pltpu.VMEM((2, PIECE, WIDE), BF16),
            pltpu.VMEM((2, PIECE, WIDE), BF16),
            pltpu.VMEM((2, 2048, WIDE), BF16),
            pltpu.VMEM((2, 512, WIDE), BF16),
            pltpu.VMEM((2, 6, 272, WIDE), I16),
            pltpu.VMEM((2, 6, 272, WIDE), I16),
            pltpu.VMEM((2, 4, 144, WIDE), I16),
            pltpu.VMEM((2, 4, 144, WIDE), I16),
            pltpu.VMEM((2, 512, WIDE), F32),
            pltpu.VMEM((2, WIDE, WIDE), F32),
            pltpu.VMEM((2, 128, WIDE), F32),
            pltpu.VMEM((2, 128, WIDE), F32),
            pltpu.VMEM((2, 15, 8, WIDE), F32),
            pltpu.VMEM((2, 8, 8, WIDE), F32),
            pltpu.VMEM((2, WIDE, WIDE), F32),
            pltpu.VMEM((2, 8, WIDE), F32),
            pltpu.SemaphoreType.DMA((9,)),
            pltpu.SemaphoreType.DMA((COPIES,)),
            pltpu.SemaphoreType.DMA((COPIES,)),
        ],
        compiler_params=pltpu.CompilerParams(
            collective_id=0, has_side_effects=True, vmem_limit_bytes=57 * 1024 * 1024),
    )(ancestor_inverse, panel, structure, diag_inverse)
    return pl.pallas_call(
        place,
        out_shape=(jax.ShapeDtypeStruct(upper.shape, BF16), jax.ShapeDtypeStruct(diagonal.shape, F32)),
        in_specs=[vmem, vmem],
        out_specs=(vmem, vmem),
        compiler_params=pltpu.CompilerParams(vmem_limit_bytes=4 * 1024 * 1024),
    )(upper, diagonal)


def solution(mesh):
    return jax.shard_map(
        local,
        mesh=mesh,
        in_specs=(P("row", "col"), P(("row", "col"), None), P(), P()),
        out_specs=(P(("row", "col"), None), P()),
        check_vma=False,
    )
```

```python
import functools

import jax
import jax.numpy as jnp
from jax import lax
from jax.experimental import pallas as pl
from jax.experimental.pallas import tpu as pltpu
from jax.sharding import PartitionSpec as P

MESH = pl.DeviceIdType.MESH
F32 = jnp.float32
BF16 = jnp.bfloat16
I16 = jnp.int16
WIDE = 256
PIECE = 128
ROUND = 12582912.0


def encode(tile, ref):
    rows = tile.shape[0]
    top = jnp.maximum(jnp.max(jnp.abs(tile), axis=0, keepdims=True), 1e-30)
    power = jnp.floor(jnp.log2(top)) - 13.0
    scaled = tile * jnp.exp2(-power)
    whole = (scaled + ROUND) - ROUND
    ref[0:rows, :] = whole.astype(jnp.int32).astype(I16)
    ref[rows:rows + 16, :] = jnp.broadcast_to(power, (16, tile.shape[1])).astype(jnp.int32).astype(I16)


def decode(ref, first=0, count=None):
    rows = ref.shape[0] - 16
    count = rows if count is None else count
    power = ref[rows:rows + 16, :].astype(jnp.int32).astype(F32)
    scale = jnp.exp2(power)[0:1, :]
    return ref[first:first + count, :].astype(jnp.int32).astype(F32) * scale


def kernel(a_hbm, panel_ref, structure_ref, upper_ref, diag_ref,
           a_v, own, neg, xb, mg, sy, ry, sz, rz, ss, dsend, drecv, xs, xr, zr,
           dg, lsem, ssem, rsem):
    R = lax.axis_index("row")
    C = lax.axis_index("col")
    x, zl, k = R // 4, (R // 2) % 2, R % 2
    y, zh = C // 4, C % 4
    z = zh * 2 + zl

    def at(dx=0, dy=0, dz=0, dzh=0, flip=False, sib=False):
        x2 = (x + dx) % 4
        y2 = (y + dy) % 4
        z2 = (z + dz + 2 * dzh) % 8
        zl2 = 1 - z2 % 2 if flip else z2 % 2
        k2 = 1 - k if sib else k
        return (x2 * 4 + zl2 * 2 + k2, y2 * 4 + z2 // 2)

    def holder(r, j):
        xs_, zls, ks = r // 4, (r // 2) % 2, r % 2
        i = (j % 4 - 2 * zls - ks + 8) % 4
        x2 = (2 * xs_ + 6 - j // 4) % 4
        upper_half = i // 2
        zl2 = jnp.where(zls == 0, (i + 1) // 2 % 2, 1 - upper_half)
        k2 = jnp.where(zls == 0, upper_half, i % 2)
        return x2 * 4 + zl2 * 2 + k2

    def piece(r, h):
        xs_, zls, ks = r // 4, (r // 2) % 2, r % 2
        x2, zl2, k2 = h // 4, (h // 2) % 2, h % 2
        i = jnp.where(zls == 0, jnp.where(zl2 == 0, 3 * k2, 1 + k2), 2 * (1 - zl2) + k2)
        return (2 * xs_ + 6 - x2) % 4 * 4 + (i + 2 * zls + ks) % 4

    ids = {}
    sends = []

    def copy(name, src, dst, dev):
        i = ids.setdefault(name, len(ids))
        return pltpu.make_async_remote_copy(
            src_ref=src, dst_ref=dst, send_sem=ssem.at[i], recv_sem=rsem.at[i],
            device_id=dev, device_id_type=MESH)

    def send(name, src, dst, dev):
        cp = copy(name, src, dst, dev)
        cp.start()
        sends.append(cp)

    def recv(name, dst):
        copy(name, dst, dst, at(sib=True)).wait_recv()

    barrier = pltpu.get_barrier_semaphore()
    target = (holder(R, C), R)
    source = (C, piece(C, R))
    plane = sorted(((d // 4, d % 4) for d in range(1, 16)),
                   key=lambda d: -min(d[0], 4 - d[0]) - min(d[1], 4 - d[1]))
    along = (4, 3, 5, 2, 6, 1, 7)
    partners = [source] + [at(dz=d) for d in along[:3]]
    partners += [at(dx=dx, dy=dy) for dx, dy in plane]
    partners += [at(dz=d) for d in along[3:]]
    partners += [at(dx=d, flip=True) for d in (1, 3)]
    partners += [at(sib=True)]
    for dev in partners:
        pl.semaphore_signal(barrier, inc=1, device_id=dev, device_id_type=MESH)
    loads = []
    for t in range(8):
        cp = pltpu.make_async_copy(a_hbm.at[pl.ds(t * 256, 256), :], a_v.at[pl.ds(t * 256, 256), :], lsem.at[t])
        cp.start()
        loads.append(cp)
    mine8 = pl.multiple_of(k * 128 + x * 32 + y * 8, 8)

    block = (R * 16 + C) // 2
    keeps = []
    for q in range(2):
        keep = structure_ref[q, block].astype(F32)
        keeps.append(keep)
        m = panel_ref[:, q * WIDE:(q + 1) * WIDE].astype(F32) * keep
        own[q] = m.astype(BF16)
        neg[q] = (-m).astype(BF16)

    pl.semaphore_wait(barrier, len(partners))

    def slot(q, s):
        return xb.at[q, pl.ds(pl.multiple_of(s * PIECE, PIECE), PIECE), :]

    def half(q, s, h):
        return xb.at[q, pl.ds(pl.multiple_of(s * PIECE + h * 64, 64), 64), :]

    def lane(dx, n, other=False):
        return piece(C, ((x + dx) % 4) * 4 + (zl + n) % 2 * 2 + (1 - k if other else k))

    def g1(q):
        send(("g1", q), neg.at[q], slot(q, C), target)

    def share(q, s, i):
        send(("gs", q, i), slot(q, s), slot(q, s), at(sib=True))

    def s1(q):
        s = lane(0, 0)
        recv(("g1", q), slot(q, s))
        names = [("xp", at(dx=1)), ("xm", at(dx=-1))]
        if q == 0:
            names += [("zp", at(dx=1, flip=True)), ("zm", at(dx=-1, flip=True))]
        names += [("z", at(flip=True))]
        for name, dev in names:
            send((name, q), slot(q, s), slot(q, s), dev)
        share(q, s, 0)

    def s2(q):
        s = lane(0, 1)
        recv(("z", q), slot(q, s))
        if q == 1:
            send(("zp", q), slot(q, s), slot(q, s), at(dx=1))
            send(("zm", q), slot(q, s), slot(q, s), at(dx=-1))
        share(q, s, 1)

    def s3(q, n):
        s = lane(1, n)
        recv(("zm" if n else "xm", q), slot(q, s))
        send(("hm", q, n), half(q, s, 0), half(q, s, 0), at(dx=-1))
        share(q, s, 2 + n)
        s = lane(-1, n)
        recv(("zp" if n else "xp", q), slot(q, s))
        send(("hp", q, n), half(q, s, 1), half(q, s, 1), at(dx=1))
        share(q, s, 4 + n)

    def s5(q, n):
        s = lane(2, n)
        recv(("hm", q, n), half(q, s, 0))
        recv(("hp", q, n), half(q, s, 1))
        share(q, s, 6 + n)

    def s6(q):
        for n in range(2):
            for i, dx in ((0, 0), (2, 1), (4, -1), (6, 2)):
                recv(("gs", q, i + n), slot(q, lane(dx, n, True)))

    def m_rows(d):
        return mg.at[:, pl.ds(pl.multiple_of(((zh + d) % 4) * PIECE, PIECE), PIECE), :]

    def m_send():
        for q in range(2):
            mg[q, pl.ds(pl.multiple_of(zh * PIECE, PIECE), PIECE), :] = own[q]
        for d in (2, 1, 3):
            send(("m", d), own, m_rows(0), at(dzh=d))

    def m_recv():
        for d in (1, 2, 3):
            recv(("m", d), m_rows(4 - d))

    def tile(q, dy, u):
        r0 = pl.multiple_of(((y + dy) % 4) * 512 + u * 256, 256)
        return jnp.dot(a_v[pl.ds(r0, 256), :], xb[q], preferred_element_type=F32)

    def y_send(q, i, value, dy):
        encode(value, sy.at[q, i])
        send(("y", q, i), sy.at[q, i], ry.at[q, i], at(dy=dy))

    def y_first(q, after):
        y_send(q, 0, tile(q, 2, 0), 1)
        after(0)
        y_send(q, 1, tile(q, 2, 1), -1)
        after(1)
        y_send(q, 2, tile(q, 1, 1), 1)
        y_send(q, 3, tile(q, -1, 0), -1)

    def y_own(q):
        for u in range(2):
            ss[q, u * 256:(u + 1) * 256, :] = tile(q, 0, u)

    def y_relay(q):
        t = tile(q, 1, 0)
        recv(("y", q, 0), ry.at[q, 0])
        y_send(q, 4, t + decode(ry.at[q, 0]), 1)
        t = tile(q, -1, 1)
        recv(("y", q, 1), ry.at[q, 1])
        y_send(q, 5, t + decode(ry.at[q, 1]), -1)

    def y_last(q):
        for i in (2, 3, 4, 5):
            recv(("y", q, i), ry.at[q, i])
        ss[q, 0:256, :] = ss[q, 0:256, :] + decode(ry.at[q, 3]) + decode(ry.at[q, 4])
        ss[q, 256:512, :] = ss[q, 256:512, :] + decode(ry.at[q, 2]) + decode(ry.at[q, 5])

    def z_ref(buf, q, i):
        return buf.at[q, i, pl.ds(0, 80 if i < 2 else 144), :]

    def z_send(q, i, value, dzh):
        encode(value, z_ref(sz, q, i))
        send(("z", q, i), z_ref(sz, q, i), z_ref(rz, q, i), at(dzh=dzh))

    def z_rows(q, d, start, count):
        r0 = pl.multiple_of(((zh + d) % 4) * PIECE + start, 64)
        return ss[q, pl.ds(r0, count), :]

    def z_first(q):
        z_send(q, 0, z_rows(q, 2, 0, 64), 1)
        z_send(q, 1, z_rows(q, 2, 64, 64), -1)

    def z_relay(q):
        recv(("z", q, 0), z_ref(rz, q, 0))
        v = jnp.concatenate([z_rows(q, 1, 0, 64) + decode(z_ref(rz, q, 0)), z_rows(q, 1, 64, 64)], axis=0)
        z_send(q, 2, v, 1)
        recv(("z", q, 1), z_ref(rz, q, 1))
        v = jnp.concatenate([z_rows(q, -1, 0, 64), z_rows(q, -1, 64, 64) + decode(z_ref(rz, q, 1))], axis=0)
        z_send(q, 3, v, -1)

    def z_last(q):
        recv(("z", q, 2), z_ref(rz, q, 2))
        recv(("z", q, 3), z_ref(rz, q, 3))
        full = z_rows(q, 0, 0, PIECE) + decode(z_ref(rz, q, 2)) + decode(z_ref(rz, q, 3))
        upper_ref[:, q * WIDE:(q + 1) * WIDE] = (full * keeps[q]).astype(BF16)

    mate = at(sib=True)

    def rows(start, count):
        return pl.ds(pl.multiple_of(start, 8), count)

    def d_core(q):
        dims = (((0,), (0,)), ((), ()))
        part = ss[q]
        high = part.astype(BF16)
        low = (part - high.astype(F32)).astype(BF16)
        dsend[q] = (lax.dot_general(mg[q], high, dims, preferred_element_type=F32)
                    + lax.dot_general(mg[q], low, dims, preferred_element_type=F32))
        send(("core", q), dsend.at[q, rows((1 - k) * 128, 128), :], drecv.at[q], mate)

    def d_plane(q):
        recv(("core", q), drecv.at[q])
        xs[q] = dsend[q, rows(k * 128, 128), :] + drecv[q]
        for i, (dx, dy) in enumerate(plane):
            r0 = ((x + dx) % 4) * 32 + ((y + dy) % 4) * 8
            send(("dp", q, i), xs.at[q, rows(r0, 8), :], xr.at[q, i], at(dx=dx, dy=dy))

    def d_z(q):
        total = xs[q, rows(x * 32 + y * 8, 8), :]
        for i in range(15):
            recv(("dp", q, i), xr.at[q, i])
            total = total + xr[q, i]
        zr[q, z] = total
        for d in along:
            send(("dz", q, d), zr.at[q, z], zr.at[q, z], at(dz=d))

    def d_back(q):
        for d in range(1, 8):
            recv(("dz", q, d), zr.at[q, (z + 8 - d) % 8])
        total = zr[q, 0]
        for i in range(1, 8):
            total = total + zr[q, i]
        dg[q, pl.ds(mine8, 8), :] = total
        part = dg.at[q, pl.ds(mine8, 8), :]
        for i, (dx, dy) in enumerate(plane):
            send(("ap", q, i), part, part, at(dx=dx, dy=dy))

    def d_back_core(q):
        for i, (dx, dy) in enumerate(plane):
            r0 = k * 128 + ((x + 4 - dx) % 4) * 32 + ((y + 4 - dy) % 4) * 8
            recv(("ap", q, i), dg.at[q, rows(r0, 8), :])
        part = dg.at[q, rows(k * 128, 128), :]
        send(("ac", q), part, part, mate)

    def d_end(q):
        recv(("ac", q), dg.at[q, rows((1 - k) * 128, 128), :])
        diag_ref[q] = dg[q]

    g1(0)
    s1(0)
    g1(1)
    s3(0, 0)
    s3(0, 1)
    s2(0)
    s5(0, 0)
    s1(1)
    s5(0, 1)
    for cp in loads:
        cp.wait()
    s6(0)
    y_first(0, lambda i: m_send() if i else s2(1))
    s3(1, 0)
    y_own(0)
    s3(1, 1)
    y_relay(0)
    s5(1, 0)
    s5(1, 1)
    s6(1)
    y_first(1, lambda i: None)
    y_own(1)
    m_recv()
    y_last(0)
    d_core(0)
    z_first(0)
    y_relay(1)
    d_plane(0)
    z_relay(0)
    d_z(0)
    y_last(1)
    d_core(1)
    z_first(1)
    z_last(0)
    d_plane(1)
    d_back(0)
    d_z(1)
    z_relay(1)
    d_back_core(0)
    z_last(1)
    d_back(1)
    d_end(0)
    d_back_core(1)
    d_end(1)
    for cp in sends:
        cp.wait_send()
    assert len(ids) <= COPIES, len(ids)


def place(upper_ref, update_ref, dinv_ref, upper_out, diag_out):
    upper_out[...] = upper_ref[...]
    diag_out[...] = dinv_ref[...] - update_ref[...]


COPIES = 160


def local(ancestor_inverse, panel, structure, diag_inverse):
    vmem = pl.BlockSpec(memory_space=pltpu.VMEM)
    hbm = pl.BlockSpec(memory_space=pltpu.HBM)
    upper, update = pl.pallas_call(
        kernel,
        out_shape=(jax.ShapeDtypeStruct(panel.shape, BF16), jax.ShapeDtypeStruct(diag_inverse.shape, F32)),
        in_specs=[hbm, vmem, pl.BlockSpec(memory_space=pltpu.SMEM)],
        out_specs=(vmem, vmem),
        scratch_shapes=[
            pltpu.VMEM((2048, 2048), BF16),
            pltpu.VMEM((2, PIECE, WIDE), BF16),
            pltpu.VMEM((2, PIECE, WIDE), BF16),
            pltpu.VMEM((2, 2048, WIDE), BF16),
            pltpu.VMEM((2, 512, WIDE), BF16),
            pltpu.VMEM((2, 6, 272, WIDE), I16),
            pltpu.VMEM((2, 6, 272, WIDE), I16),
            pltpu.VMEM((2, 4, 144, WIDE), I16),
            pltpu.VMEM((2, 4, 144, WIDE), I16),
            pltpu.VMEM((2, 512, WIDE), F32),
            pltpu.VMEM((2, WIDE, WIDE), F32),
            pltpu.VMEM((2, 128, WIDE), F32),
            pltpu.VMEM((2, 128, WIDE), F32),
            pltpu.VMEM((2, 15, 8, WIDE), F32),
            pltpu.VMEM((2, 8, 8, WIDE), F32),
            pltpu.VMEM((2, WIDE, WIDE), F32),
            pltpu.SemaphoreType.DMA((8,)),
            pltpu.SemaphoreType.DMA((COPIES,)),
            pltpu.SemaphoreType.DMA((COPIES,)),
        ],
        compiler_params=pltpu.CompilerParams(
            collective_id=0, has_side_effects=True, vmem_limit_bytes=52 * 1024 * 1024),
    )(ancestor_inverse, panel, structure)
    return pl.pallas_call(
        place,
        out_shape=(jax.ShapeDtypeStruct(upper.shape, BF16), jax.ShapeDtypeStruct(update.shape, F32)),
        in_specs=[vmem, vmem, vmem],
        out_specs=(vmem, vmem),
        compiler_params=pltpu.CompilerParams(vmem_limit_bytes=4 * 1024 * 1024),
    )(upper, update, diag_inverse)


def solution(mesh):
    return jax.shard_map(
        local,
        mesh=mesh,
        in_specs=(P("row", "col"), P(("row", "col"), None), P(), P()),
        out_specs=(P(("row", "col"), None), P()),
        check_vma=False,
    )
```

```python
import functools

import jax
import jax.numpy as jnp
from jax import lax
from jax.experimental import pallas as pl
from jax.experimental.pallas import tpu as pltpu
from jax.sharding import PartitionSpec as P

MESH = pl.DeviceIdType.MESH
F32 = jnp.float32
BF16 = jnp.bfloat16
I16 = jnp.int16
WIDE = 256
PIECE = 128
ROUND = 12582912.0


def encode(tile, ref):
    rows = tile.shape[0]
    top = jnp.maximum(jnp.max(jnp.abs(tile), axis=0, keepdims=True), 1e-30)
    power = jnp.floor(jnp.log2(top)) - 13.0
    scaled = tile * jnp.exp2(-power)
    whole = (scaled + ROUND) - ROUND
    ref[0:rows, :] = whole.astype(jnp.int32).astype(I16)
    ref[rows:rows + 16, :] = jnp.broadcast_to(power, (16, tile.shape[1])).astype(jnp.int32).astype(I16)


def decode(ref, first=0, count=None):
    rows = ref.shape[0] - 16
    count = rows if count is None else count
    power = ref[rows:rows + 16, :].astype(jnp.int32).astype(F32)
    scale = jnp.exp2(power)[0:1, :]
    return ref[first:first + count, :].astype(jnp.int32).astype(F32) * scale


def kernel(a_hbm, panel_ref, structure_ref, upper_ref, diag_ref,
           a_v, own, neg, xb, mg, sy, ry, sz, rz, ss, dsend, drecv, xs, xr, zr,
           dg, lsem, ssem, rsem):
    R = lax.axis_index("row")
    C = lax.axis_index("col")
    x, zl, k = R // 4, (R // 2) % 2, R % 2
    y, zh = C // 4, C % 4
    z = zh * 2 + zl

    def at(dx=0, dy=0, dz=0, dzh=0, flip=False, sib=False):
        x2 = (x + dx) % 4
        y2 = (y + dy) % 4
        z2 = (z + dz + 2 * dzh) % 8
        zl2 = 1 - z2 % 2 if flip else z2 % 2
        k2 = 1 - k if sib else k
        return (x2 * 4 + zl2 * 2 + k2, y2 * 4 + z2 // 2)

    def holder(r, j):
        xs_, zls, ks = r // 4, (r // 2) % 2, r % 2
        i = (j % 4 - 2 * zls - ks + 8) % 4
        x2 = (2 * xs_ + 6 - j // 4) % 4
        upper_half = i // 2
        zl2 = jnp.where(zls == 0, (i + 1) // 2 % 2, 1 - upper_half)
        k2 = jnp.where(zls == 0, upper_half, i % 2)
        return x2 * 4 + zl2 * 2 + k2

    def piece(r, h):
        xs_, zls, ks = r // 4, (r // 2) % 2, r % 2
        x2, zl2, k2 = h // 4, (h // 2) % 2, h % 2
        i = jnp.where(zls == 0, jnp.where(zl2 == 0, 3 * k2, 1 + k2), 2 * (1 - zl2) + k2)
        return (2 * xs_ + 6 - x2) % 4 * 4 + (i + 2 * zls + ks) % 4

    ids = {}
    sends = []

    def copy(name, src, dst, dev):
        i = ids.setdefault(name, len(ids))
        return pltpu.make_async_remote_copy(
            src_ref=src, dst_ref=dst, send_sem=ssem.at[i], recv_sem=rsem.at[i],
            device_id=dev, device_id_type=MESH)

    def send(name, src, dst, dev):
        cp = copy(name, src, dst, dev)
        cp.start()
        sends.append(cp)

    def recv(name, dst):
        copy(name, dst, dst, at(sib=True)).wait_recv()

    barrier = pltpu.get_barrier_semaphore()
    target = (holder(R, C), R)
    source = (C, piece(C, R))
    plane = sorted(((d // 4, d % 4) for d in range(1, 16)),
                   key=lambda d: -min(d[0], 4 - d[0]) - min(d[1], 4 - d[1]))
    along = (4, 3, 5, 2, 6, 1, 7)
    partners = [source] + [at(dz=d) for d in along[:3]]
    partners += [at(dx=dx, dy=dy) for dx, dy in plane]
    partners += [at(dz=d) for d in along[3:]]
    partners += [at(dx=d, flip=True) for d in (1, 3)]
    partners += [at(sib=True)]
    for dev in partners:
        pl.semaphore_signal(barrier, inc=1, device_id=dev, device_id_type=MESH)
    loads = []
    for t in range(8):
        cp = pltpu.make_async_copy(a_hbm.at[pl.ds(t * 256, 256), :], a_v.at[pl.ds(t * 256, 256), :], lsem.at[t])
        cp.start()
        loads.append(cp)
    mine8 = pl.multiple_of(k * 128 + x * 32 + y * 8, 8)

    block = (R * 16 + C) // 2
    keeps = []
    for q in range(2):
        keep = structure_ref[q, block].astype(F32)
        keeps.append(keep)
        m = panel_ref[:, q * WIDE:(q + 1) * WIDE].astype(F32) * keep
        own[q] = m.astype(BF16)
        neg[q] = (-m).astype(BF16)

    pl.semaphore_wait(barrier, len(partners))

    def slot(q, s):
        return xb.at[q, pl.ds(pl.multiple_of(s * PIECE, PIECE), PIECE), :]

    def half(q, s, h):
        return xb.at[q, pl.ds(pl.multiple_of(s * PIECE + h * 64, 64), 64), :]

    def lane(dx, n, other=False):
        return piece(C, ((x + dx) % 4) * 4 + (zl + n) % 2 * 2 + (1 - k if other else k))

    def g1(q):
        send(("g1", q), neg.at[q], slot(q, C), target)

    def share(q, s, i):
        send(("gs", q, i), slot(q, s), slot(q, s), at(sib=True))

    def s1(q):
        s = lane(0, 0)
        recv(("g1", q), slot(q, s))
        names = [("xp", at(dx=1)), ("xm", at(dx=-1))]
        if q == 0:
            names += [("zp", at(dx=1, flip=True)), ("zm", at(dx=-1, flip=True))]
        names += [("z", at(flip=True))]
        for name, dev in names:
            send((name, q), slot(q, s), slot(q, s), dev)
        share(q, s, 0)

    def s2(q):
        s = lane(0, 1)
        recv(("z", q), slot(q, s))
        if q == 1:
            send(("zp", q), slot(q, s), slot(q, s), at(dx=1))
            send(("zm", q), slot(q, s), slot(q, s), at(dx=-1))
        share(q, s, 1)

    def s3(q, n):
        s = lane(1, n)
        recv(("zm" if n else "xm", q), slot(q, s))
        send(("hm", q, n), half(q, s, 0), half(q, s, 0), at(dx=-1))
        share(q, s, 2 + n)
        s = lane(-1, n)
        recv(("zp" if n else "xp", q), slot(q, s))
        send(("hp", q, n), half(q, s, 1), half(q, s, 1), at(dx=1))
        share(q, s, 4 + n)

    def s5(q, n):
        s = lane(2, n)
        recv(("hm", q, n), half(q, s, 0))
        recv(("hp", q, n), half(q, s, 1))
        share(q, s, 6 + n)

    def s6(q):
        for n in range(2):
            for i, dx in ((0, 0), (2, 1), (4, -1), (6, 2)):
                recv(("gs", q, i + n), slot(q, lane(dx, n, True)))

    def m_rows(d):
        return mg.at[:, pl.ds(pl.multiple_of(((zh + d) % 4) * PIECE, PIECE), PIECE), :]

    def m_send():
        for q in range(2):
            mg[q, pl.ds(pl.multiple_of(zh * PIECE, PIECE), PIECE), :] = own[q]
        for d in (2, 1, 3):
            send(("m", d), own, m_rows(0), at(dzh=d))

    def m_recv():
        for d in (1, 2, 3):
            recv(("m", d), m_rows(4 - d))

    def tile(q, dy, u):
        r0 = pl.multiple_of(((y + dy) % 4) * 512 + u * 256, 256)
        return jnp.dot(a_v[pl.ds(r0, 256), :], xb[q], preferred_element_type=F32)

    def y_send(q, i, value, dy):
        encode(value, sy.at[q, i])
        send(("y", q, i), sy.at[q, i], ry.at[q, i], at(dy=dy))

    def y_first(q, after):
        y_send(q, 0, tile(q, 2, 0), 1)
        after(0)
        y_send(q, 1, tile(q, 2, 1), -1)
        after(1)
        y_send(q, 2, tile(q, 1, 1), 1)
        y_send(q, 3, tile(q, -1, 0), -1)

    def y_own(q):
        for u in range(2):
            ss[q, u * 256:(u + 1) * 256, :] = tile(q, 0, u)

    def y_relay(q):
        t = tile(q, 1, 0)
        recv(("y", q, 0), ry.at[q, 0])
        y_send(q, 4, t + decode(ry.at[q, 0]), 1)
        t = tile(q, -1, 1)
        recv(("y", q, 1), ry.at[q, 1])
        y_send(q, 5, t + decode(ry.at[q, 1]), -1)

    def y_last(q):
        for i in (2, 3, 4, 5):
            recv(("y", q, i), ry.at[q, i])
        ss[q, 0:256, :] = ss[q, 0:256, :] + decode(ry.at[q, 3]) + decode(ry.at[q, 4])
        ss[q, 256:512, :] = ss[q, 256:512, :] + decode(ry.at[q, 2]) + decode(ry.at[q, 5])

    def z_ref(buf, q, i):
        return buf.at[q, i, pl.ds(0, 80 if i < 2 else 144), :]

    def z_send(q, i, value, dzh):
        encode(value, z_ref(sz, q, i))
        send(("z", q, i), z_ref(sz, q, i), z_ref(rz, q, i), at(dzh=dzh))

    def z_rows(q, d, start, count):
        r0 = pl.multiple_of(((zh + d) % 4) * PIECE + start, 64)
        return ss[q, pl.ds(r0, count), :]

    def z_first(q):
        z_send(q, 0, z_rows(q, 2, 0, 64), 1)
        z_send(q, 1, z_rows(q, 2, 64, 64), -1)

    def z_relay(q):
        recv(("z", q, 0), z_ref(rz, q, 0))
        v = jnp.concatenate([z_rows(q, 1, 0, 64) + decode(z_ref(rz, q, 0)), z_rows(q, 1, 64, 64)], axis=0)
        z_send(q, 2, v, 1)
        recv(("z", q, 1), z_ref(rz, q, 1))
        v = jnp.concatenate([z_rows(q, -1, 0, 64), z_rows(q, -1, 64, 64) + decode(z_ref(rz, q, 1))], axis=0)
        z_send(q, 3, v, -1)

    def z_last(q):
        recv(("z", q, 2), z_ref(rz, q, 2))
        recv(("z", q, 3), z_ref(rz, q, 3))
        full = z_rows(q, 0, 0, PIECE) + decode(z_ref(rz, q, 2)) + decode(z_ref(rz, q, 3))
        upper_ref[:, q * WIDE:(q + 1) * WIDE] = (full * keeps[q]).astype(BF16)

    mate = at(sib=True)

    def rows(start, count):
        return pl.ds(pl.multiple_of(start, 8), count)

    def d_core(q):
        dims = (((0,), (0,)), ((), ()))
        part = ss[q]
        high = part.astype(BF16)
        low = (part - high.astype(F32)).astype(BF16)
        dsend[q] = (lax.dot_general(mg[q], high, dims, preferred_element_type=F32)
                    + lax.dot_general(mg[q], low, dims, preferred_element_type=F32))
        send(("core", q), dsend.at[q, rows((1 - k) * 128, 128), :], drecv.at[q], mate)

    def d_plane(q):
        recv(("core", q), drecv.at[q])
        xs[q] = dsend[q, rows(k * 128, 128), :] + drecv[q]
        for i, (dx, dy) in enumerate(plane):
            r0 = ((x + dx) % 4) * 32 + ((y + dy) % 4) * 8
            send(("dp", q, i), xs.at[q, rows(r0, 8), :], xr.at[q, i], at(dx=dx, dy=dy))

    def d_z(q):
        total = xs[q, rows(x * 32 + y * 8, 8), :]
        for i in range(15):
            recv(("dp", q, i), xr.at[q, i])
            total = total + xr[q, i]
        zr[q, z] = total
        for d in along:
            send(("dz", q, d), zr.at[q, z], zr.at[q, z], at(dz=d))

    def d_back(q):
        for d in range(1, 8):
            recv(("dz", q, d), zr.at[q, (z + 8 - d) % 8])
        total = zr[q, 0]
        for i in range(1, 8):
            total = total + zr[q, i]
        dg[q, pl.ds(mine8, 8), :] = total
        part = dg.at[q, pl.ds(mine8, 8), :]
        for i, (dx, dy) in enumerate(plane):
            send(("ap", q, i), part, part, at(dx=dx, dy=dy))

    def d_back_core(q):
        for i, (dx, dy) in enumerate(plane):
            r0 = k * 128 + ((x + 4 - dx) % 4) * 32 + ((y + 4 - dy) % 4) * 8
            recv(("ap", q, i), dg.at[q, rows(r0, 8), :])
        part = dg.at[q, rows(k * 128, 128), :]
        send(("ac", q), part, part, mate)

    def d_end(q):
        recv(("ac", q), dg.at[q, rows((1 - k) * 128, 128), :])
        diag_ref[q] = dg[q]

    g1(0)
    s1(0)
    g1(1)
    s3(0, 0)
    s3(0, 1)
    s2(0)
    s5(0, 0)
    s1(1)
    s5(0, 1)
    for cp in loads:
        cp.wait()
    s6(0)
    y_first(0, lambda i: m_send() if i else s2(1))
    s3(1, 0)
    y_own(0)
    s3(1, 1)
    y_relay(0)
    s5(1, 0)
    s5(1, 1)
    s6(1)
    y_first(1, lambda i: None)
    y_own(1)
    m_recv()
    y_last(0)
    d_core(0)
    z_first(0)
    y_relay(1)
    d_plane(0)
    z_relay(0)
    d_z(0)
    y_last(1)
    d_core(1)
    z_first(1)
    d_plane(1)
    z_last(0)
    d_back(0)
    d_z(1)
    z_relay(1)
    d_back_core(0)
    d_back(1)
    d_end(0)
    d_back_core(1)
    z_last(1)
    d_end(1)
    for cp in sends:
        cp.wait_send()
    assert len(ids) <= COPIES, len(ids)


def place(upper_ref, update_ref, dinv_ref, upper_out, diag_out):
    upper_out[...] = upper_ref[...]
    diag_out[...] = dinv_ref[...] - update_ref[...]


COPIES = 160


def local(ancestor_inverse, panel, structure, diag_inverse):
    vmem = pl.BlockSpec(memory_space=pltpu.VMEM)
    hbm = pl.BlockSpec(memory_space=pltpu.HBM)
    upper, update = pl.pallas_call(
        kernel,
        out_shape=(jax.ShapeDtypeStruct(panel.shape, BF16), jax.ShapeDtypeStruct(diag_inverse.shape, F32)),
        in_specs=[hbm, vmem, pl.BlockSpec(memory_space=pltpu.SMEM)],
        out_specs=(vmem, vmem),
        scratch_shapes=[
            pltpu.VMEM((2048, 2048), BF16),
            pltpu.VMEM((2, PIECE, WIDE), BF16),
            pltpu.VMEM((2, PIECE, WIDE), BF16),
            pltpu.VMEM((2, 2048, WIDE), BF16),
            pltpu.VMEM((2, 512, WIDE), BF16),
            pltpu.VMEM((2, 6, 272, WIDE), I16),
            pltpu.VMEM((2, 6, 272, WIDE), I16),
            pltpu.VMEM((2, 4, 144, WIDE), I16),
            pltpu.VMEM((2, 4, 144, WIDE), I16),
            pltpu.VMEM((2, 512, WIDE), F32),
            pltpu.VMEM((2, WIDE, WIDE), F32),
            pltpu.VMEM((2, 128, WIDE), F32),
            pltpu.VMEM((2, 128, WIDE), F32),
            pltpu.VMEM((2, 15, 8, WIDE), F32),
            pltpu.VMEM((2, 8, 8, WIDE), F32),
            pltpu.VMEM((2, WIDE, WIDE), F32),
            pltpu.SemaphoreType.DMA((8,)),
            pltpu.SemaphoreType.DMA((COPIES,)),
            pltpu.SemaphoreType.DMA((COPIES,)),
        ],
        compiler_params=pltpu.CompilerParams(
            collective_id=0, has_side_effects=True, vmem_limit_bytes=52 * 1024 * 1024),
    )(ancestor_inverse, panel, structure)
    return pl.pallas_call(
        place,
        out_shape=(jax.ShapeDtypeStruct(upper.shape, BF16), jax.ShapeDtypeStruct(update.shape, F32)),
        in_specs=[vmem, vmem, vmem],
        out_specs=(vmem, vmem),
        compiler_params=pltpu.CompilerParams(vmem_limit_bytes=4 * 1024 * 1024),
    )(upper, update, diag_inverse)


def solution(mesh):
    return jax.shard_map(
        local,
        mesh=mesh,
        in_specs=(P("row", "col"), P(("row", "col"), None), P(), P()),
        out_specs=(P(("row", "col"), None), P()),
        check_vma=False,
    )
```

```python
import functools

import jax
import jax.numpy as jnp
from jax import lax
from jax.experimental import pallas as pl
from jax.experimental.pallas import tpu as pltpu
from jax.sharding import PartitionSpec as P

MESH = pl.DeviceIdType.MESH
F32 = jnp.float32
BF16 = jnp.bfloat16
I16 = jnp.int16
WIDE = 256
PIECE = 128
ROUND = 12582912.0


def encode(tile, ref):
    rows = tile.shape[0]
    top = jnp.maximum(jnp.max(jnp.abs(tile), axis=0, keepdims=True), 1e-30)
    power = jnp.floor(jnp.log2(top)) - 13.0
    scaled = tile * jnp.exp2(-power)
    whole = (scaled + ROUND) - ROUND
    ref[0:rows, :] = whole.astype(jnp.int32).astype(I16)
    ref[rows:rows + 16, :] = jnp.broadcast_to(power, (16, tile.shape[1])).astype(jnp.int32).astype(I16)


def decode(ref, first=0, count=None):
    rows = ref.shape[0] - 16
    count = rows if count is None else count
    power = ref[rows:rows + 16, :].astype(jnp.int32).astype(F32)
    scale = jnp.exp2(power)[0:1, :]
    return ref[first:first + count, :].astype(jnp.int32).astype(F32) * scale


def kernel(a_hbm, panel_ref, structure_ref, upper_ref, diag_ref,
           a_v, own, neg, xb, mg, sy, ry, sz, rz, ss, dsend, drecv, xs, xr, zr,
           dg, lsem, ssem, rsem):
    R = lax.axis_index("row")
    C = lax.axis_index("col")
    x, zl, k = R // 4, (R // 2) % 2, R % 2
    y, zh = C // 4, C % 4
    z = zh * 2 + zl

    def at(dx=0, dy=0, dz=0, dzh=0, flip=False, sib=False):
        x2 = (x + dx) % 4
        y2 = (y + dy) % 4
        z2 = (z + dz + 2 * dzh) % 8
        zl2 = 1 - z2 % 2 if flip else z2 % 2
        k2 = 1 - k if sib else k
        return (x2 * 4 + zl2 * 2 + k2, y2 * 4 + z2 // 2)

    def holder(r, j):
        xs_, zls, ks = r // 4, (r // 2) % 2, r % 2
        i = (j % 4 - 2 * zls - ks + 8) % 4
        x2 = (2 * xs_ + 6 - j // 4) % 4
        upper_half = i // 2
        zl2 = jnp.where(zls == 0, (i + 1) // 2 % 2, 1 - upper_half)
        k2 = jnp.where(zls == 0, upper_half, i % 2)
        return x2 * 4 + zl2 * 2 + k2

    def piece(r, h):
        xs_, zls, ks = r // 4, (r // 2) % 2, r % 2
        x2, zl2, k2 = h // 4, (h // 2) % 2, h % 2
        i = jnp.where(zls == 0, jnp.where(zl2 == 0, 3 * k2, 1 + k2), 2 * (1 - zl2) + k2)
        return (2 * xs_ + 6 - x2) % 4 * 4 + (i + 2 * zls + ks) % 4

    ids = {}
    sends = []

    def copy(name, src, dst, dev):
        i = ids.setdefault(name, len(ids))
        return pltpu.make_async_remote_copy(
            src_ref=src, dst_ref=dst, send_sem=ssem.at[i], recv_sem=rsem.at[i],
            device_id=dev, device_id_type=MESH)

    def send(name, src, dst, dev):
        cp = copy(name, src, dst, dev)
        cp.start()
        sends.append(cp)

    def recv(name, dst):
        copy(name, dst, dst, at(sib=True)).wait_recv()

    barrier = pltpu.get_barrier_semaphore()
    target = (holder(R, C), R)
    source = (C, piece(C, R))
    plane = sorted(((d // 4, d % 4) for d in range(1, 16)),
                   key=lambda d: -min(d[0], 4 - d[0]) - min(d[1], 4 - d[1]))
    along = (4, 3, 5, 2, 6, 1, 7)
    partners = [source] + [at(dz=d) for d in along[:3]]
    partners += [at(dx=dx, dy=dy) for dx, dy in plane]
    partners += [at(dz=d) for d in along[3:]]
    partners += [at(dx=d, flip=True) for d in (1, 3)]
    partners += [at(sib=True)]
    for dev in partners:
        pl.semaphore_signal(barrier, inc=1, device_id=dev, device_id_type=MESH)
    loads = []
    for t in range(8):
        cp = pltpu.make_async_copy(a_hbm.at[pl.ds(t * 256, 256), :], a_v.at[pl.ds(t * 256, 256), :], lsem.at[t])
        cp.start()
        loads.append(cp)
    mine8 = pl.multiple_of(k * 128 + x * 32 + y * 8, 8)

    block = (R * 16 + C) // 2
    keeps = []
    for q in range(2):
        keep = structure_ref[q, block].astype(F32)
        keeps.append(keep)
        m = panel_ref[:, q * WIDE:(q + 1) * WIDE].astype(F32) * keep
        own[q] = m.astype(BF16)
        neg[q] = (-m).astype(BF16)

    pl.semaphore_wait(barrier, len(partners))

    def slot(q, s):
        return xb.at[q, pl.ds(pl.multiple_of(s * PIECE, PIECE), PIECE), :]

    def half(q, s, h):
        return xb.at[q, pl.ds(pl.multiple_of(s * PIECE + h * 64, 64), 64), :]

    def lane(dx, n, other=False):
        return piece(C, ((x + dx) % 4) * 4 + (zl + n) % 2 * 2 + (1 - k if other else k))

    def g1(q):
        send(("g1", q), neg.at[q], slot(q, C), target)

    def share(q, s, i):
        send(("gs", q, i), slot(q, s), slot(q, s), at(sib=True))

    def s1(q):
        s = lane(0, 0)
        recv(("g1", q), slot(q, s))
        names = [("xp", at(dx=1)), ("xm", at(dx=-1))]
        if q == 0:
            names += [("zp", at(dx=1, flip=True)), ("zm", at(dx=-1, flip=True))]
        names += [("z", at(flip=True))]
        for name, dev in names:
            send((name, q), slot(q, s), slot(q, s), dev)
        share(q, s, 0)

    def s2(q):
        s = lane(0, 1)
        recv(("z", q), slot(q, s))
        if q == 1:
            send(("zp", q), slot(q, s), slot(q, s), at(dx=1))
            send(("zm", q), slot(q, s), slot(q, s), at(dx=-1))
        share(q, s, 1)

    def s3(q, n):
        s = lane(1, n)
        recv(("zm" if n else "xm", q), slot(q, s))
        send(("hm", q, n), half(q, s, 0), half(q, s, 0), at(dx=-1))
        share(q, s, 2 + n)
        s = lane(-1, n)
        recv(("zp" if n else "xp", q), slot(q, s))
        send(("hp", q, n), half(q, s, 1), half(q, s, 1), at(dx=1))
        share(q, s, 4 + n)

    def s5(q, n):
        s = lane(2, n)
        recv(("hm", q, n), half(q, s, 0))
        recv(("hp", q, n), half(q, s, 1))
        share(q, s, 6 + n)

    def s6(q):
        for n in range(2):
            for i, dx in ((0, 0), (2, 1), (4, -1), (6, 2)):
                recv(("gs", q, i + n), slot(q, lane(dx, n, True)))

    def m_rows(d):
        return mg.at[:, pl.ds(pl.multiple_of(((zh + d) % 4) * PIECE, PIECE), PIECE), :]

    def m_send():
        for q in range(2):
            mg[q, pl.ds(pl.multiple_of(zh * PIECE, PIECE), PIECE), :] = own[q]
        for d in (2, 1, 3):
            send(("m", d), own, m_rows(0), at(dzh=d))

    def m_recv():
        for d in (1, 2, 3):
            recv(("m", d), m_rows(4 - d))

    def tile(q, dy, u):
        r0 = pl.multiple_of(((y + dy) % 4) * 512 + u * 256, 256)
        return jnp.dot(a_v[pl.ds(r0, 256), :], xb[q], preferred_element_type=F32)

    def y_send(q, i, value, dy):
        encode(value, sy.at[q, i])
        send(("y", q, i), sy.at[q, i], ry.at[q, i], at(dy=dy))

    def y_first(q, after):
        y_send(q, 0, tile(q, 2, 0), 1)
        after(0)
        y_send(q, 1, tile(q, 2, 1), -1)
        after(1)
        y_send(q, 2, tile(q, 1, 1), 1)
        y_send(q, 3, tile(q, -1, 0), -1)

    def y_own(q):
        for u in range(2):
            ss[q, u * 256:(u + 1) * 256, :] = tile(q, 0, u)

    def y_relay(q):
        t = tile(q, 1, 0)
        recv(("y", q, 0), ry.at[q, 0])
        y_send(q, 4, t + decode(ry.at[q, 0]), 1)
        t = tile(q, -1, 1)
        recv(("y", q, 1), ry.at[q, 1])
        y_send(q, 5, t + decode(ry.at[q, 1]), -1)

    def y_last(q):
        for i in (2, 3, 4, 5):
            recv(("y", q, i), ry.at[q, i])
        ss[q, 0:256, :] = ss[q, 0:256, :] + decode(ry.at[q, 3]) + decode(ry.at[q, 4])
        ss[q, 256:512, :] = ss[q, 256:512, :] + decode(ry.at[q, 2]) + decode(ry.at[q, 5])

    def z_ref(buf, q, i):
        return buf.at[q, i, pl.ds(0, 80 if i < 2 else 144), :]

    def z_send(q, i, value, dzh):
        encode(value, z_ref(sz, q, i))
        send(("z", q, i), z_ref(sz, q, i), z_ref(rz, q, i), at(dzh=dzh))

    def z_rows(q, d, start, count):
        r0 = pl.multiple_of(((zh + d) % 4) * PIECE + start, 64)
        return ss[q, pl.ds(r0, count), :]

    def z_first(q):
        z_send(q, 0, z_rows(q, 2, 0, 64), 1)
        z_send(q, 1, z_rows(q, 2, 64, 64), -1)

    def z_relay(q):
        recv(("z", q, 0), z_ref(rz, q, 0))
        v = jnp.concatenate([z_rows(q, 1, 0, 64) + decode(z_ref(rz, q, 0)), z_rows(q, 1, 64, 64)], axis=0)
        z_send(q, 2, v, 1)
        recv(("z", q, 1), z_ref(rz, q, 1))
        v = jnp.concatenate([z_rows(q, -1, 0, 64), z_rows(q, -1, 64, 64) + decode(z_ref(rz, q, 1))], axis=0)
        z_send(q, 3, v, -1)

    def z_last(q):
        recv(("z", q, 2), z_ref(rz, q, 2))
        recv(("z", q, 3), z_ref(rz, q, 3))
        full = z_rows(q, 0, 0, PIECE) + decode(z_ref(rz, q, 2)) + decode(z_ref(rz, q, 3))
        upper_ref[:, q * WIDE:(q + 1) * WIDE] = (full * keeps[q]).astype(BF16)

    mate = at(sib=True)

    def rows(start, count):
        return pl.ds(pl.multiple_of(start, 8), count)

    def d_core(q):
        dims = (((0,), (0,)), ((), ()))
        part = ss[q]
        high = part.astype(BF16)
        low = (part - high.astype(F32)).astype(BF16)
        dsend[q] = (lax.dot_general(mg[q], high, dims, preferred_element_type=F32)
                    + lax.dot_general(mg[q], low, dims, preferred_element_type=F32))
        send(("core", q), dsend.at[q, rows((1 - k) * 128, 128), :], drecv.at[q], mate)

    def d_plane(q):
        recv(("core", q), drecv.at[q])
        xs[q] = dsend[q, rows(k * 128, 128), :] + drecv[q]
        for i, (dx, dy) in enumerate(plane):
            r0 = ((x + dx) % 4) * 32 + ((y + dy) % 4) * 8
            send(("dp", q, i), xs.at[q, rows(r0, 8), :], xr.at[q, i], at(dx=dx, dy=dy))

    def d_z(q):
        total = xs[q, rows(x * 32 + y * 8, 8), :]
        for i in range(15):
            recv(("dp", q, i), xr.at[q, i])
            total = total + xr[q, i]
        zr[q, z] = total
        for d in along:
            send(("dz", q, d), zr.at[q, z], zr.at[q, z], at(dz=d))

    def d_back(q):
        for d in range(1, 8):
            recv(("dz", q, d), zr.at[q, (z + 8 - d) % 8])
        total = zr[q, 0]
        for i in range(1, 8):
            total = total + zr[q, i]
        dg[q, pl.ds(mine8, 8), :] = total
        part = dg.at[q, pl.ds(mine8, 8), :]
        for i, (dx, dy) in enumerate(plane):
            send(("ap", q, i), part, part, at(dx=dx, dy=dy))

    def d_back_core(q):
        for i, (dx, dy) in enumerate(plane):
            r0 = k * 128 + ((x + 4 - dx) % 4) * 32 + ((y + 4 - dy) % 4) * 8
            recv(("ap", q, i), dg.at[q, rows(r0, 8), :])
        part = dg.at[q, rows(k * 128, 128), :]
        send(("ac", q), part, part, mate)

    def d_end(q):
        recv(("ac", q), dg.at[q, rows((1 - k) * 128, 128), :])
        diag_ref[q] = dg[q]

    g1(0)
    s1(0)
    g1(1)
    s3(0, 0)
    s3(0, 1)
    s1(1)
    s2(0)
    s5(0, 0)
    s5(0, 1)
    for cp in loads:
        cp.wait()
    s6(0)
    y_first(0, lambda i: m_send() if i else s2(1))
    s3(1, 0)
    y_own(0)
    s3(1, 1)
    y_relay(0)
    s5(1, 0)
    s5(1, 1)
    s6(1)
    y_first(1, lambda i: None)
    y_own(1)
    m_recv()
    y_last(0)
    d_core(0)
    z_first(0)
    y_relay(1)
    d_plane(0)
    z_relay(0)
    d_z(0)
    y_last(1)
    d_core(1)
    z_first(1)
    d_plane(1)
    z_last(0)
    d_back(0)
    d_z(1)
    z_relay(1)
    d_back_core(0)
    d_back(1)
    d_end(0)
    d_back_core(1)
    z_last(1)
    d_end(1)
    for cp in sends:
        cp.wait_send()
    assert len(ids) <= COPIES, len(ids)


def place(upper_ref, update_ref, dinv_ref, upper_out, diag_out):
    upper_out[...] = upper_ref[...]
    diag_out[...] = dinv_ref[...] - update_ref[...]


COPIES = 160


def local(ancestor_inverse, panel, structure, diag_inverse):
    vmem = pl.BlockSpec(memory_space=pltpu.VMEM)
    hbm = pl.BlockSpec(memory_space=pltpu.HBM)
    upper, update = pl.pallas_call(
        kernel,
        out_shape=(jax.ShapeDtypeStruct(panel.shape, BF16), jax.ShapeDtypeStruct(diag_inverse.shape, F32)),
        in_specs=[hbm, vmem, pl.BlockSpec(memory_space=pltpu.SMEM)],
        out_specs=(vmem, vmem),
        scratch_shapes=[
            pltpu.VMEM((2048, 2048), BF16),
            pltpu.VMEM((2, PIECE, WIDE), BF16),
            pltpu.VMEM((2, PIECE, WIDE), BF16),
            pltpu.VMEM((2, 2048, WIDE), BF16),
            pltpu.VMEM((2, 512, WIDE), BF16),
            pltpu.VMEM((2, 6, 272, WIDE), I16),
            pltpu.VMEM((2, 6, 272, WIDE), I16),
            pltpu.VMEM((2, 4, 144, WIDE), I16),
            pltpu.VMEM((2, 4, 144, WIDE), I16),
            pltpu.VMEM((2, 512, WIDE), F32),
            pltpu.VMEM((2, WIDE, WIDE), F32),
            pltpu.VMEM((2, 128, WIDE), F32),
            pltpu.VMEM((2, 128, WIDE), F32),
            pltpu.VMEM((2, 15, 8, WIDE), F32),
            pltpu.VMEM((2, 8, 8, WIDE), F32),
            pltpu.VMEM((2, WIDE, WIDE), F32),
            pltpu.SemaphoreType.DMA((8,)),
            pltpu.SemaphoreType.DMA((COPIES,)),
            pltpu.SemaphoreType.DMA((COPIES,)),
        ],
        compiler_params=pltpu.CompilerParams(
            collective_id=0, has_side_effects=True, vmem_limit_bytes=52 * 1024 * 1024),
    )(ancestor_inverse, panel, structure)
    return pl.pallas_call(
        place,
        out_shape=(jax.ShapeDtypeStruct(upper.shape, BF16), jax.ShapeDtypeStruct(update.shape, F32)),
        in_specs=[vmem, vmem, vmem],
        out_specs=(vmem, vmem),
        compiler_params=pltpu.CompilerParams(vmem_limit_bytes=4 * 1024 * 1024),
    )(upper, update, diag_inverse)


def solution(mesh):
    return jax.shard_map(
        local,
        mesh=mesh,
        in_specs=(P("row", "col"), P(("row", "col"), None), P(), P()),
        out_specs=(P(("row", "col"), None), P()),
        check_vma=False,
    )
```
